32 devices in a mesh: grp: 4 (over z), dev: 8 (over y, x, core).
Axes of the slice: x: 2, y: 2, z: 4, core: 2. Of those that a mesh axis runs over, the one named last changes fastest.
Arguments:
- panel: float32 [32768, 512], P(('grp', 'dev')), may hold values from -45 to 45
- signs: int32 [32768], P(('grp', 'dev')), may hold values from 0 to 1
- source_group: int32 [4, 8, 32, 1], P(None, 'dev'), may hold values from 0 to 3; in each aligned block of 32 rows (0 to 31, 32 to 63, ..., all dimensions but the last counted through in order) at most 16 rows name the same one
- source_row: int32 [4, 8, 32], P(None, 'dev'), may hold values from 0 to 1023, as said below
Outputs:
- sketch: float32 [1024, 512], P(('grp', 'dev'))
- conditioned: float32 [32768, 512], P(('grp', 'dev'))
The draws below stay inside these ranges and needn't reach their ends.
Inputs may be any that keep to these rules, and one draw needn't show every extreme that they name: Among the 32 entries source_group[g, d, :, 0] for one g and d, no group is named more than 16 times, and in some such block one group is named exactly 16 times. source_row[g, d, j] lies in the row band of owner j // 4: source_row[g, d, j] // 128 equals j // 4; the row within the band is free.
All inputs are finite; a program needn't handle non-finite values.
Results may differ from the reference program's by a relative error of at most 0.00013.
Values sent between devices are 32-bit elements; how exact they have to be, the bound alone decides.
A program may use at most 64 MiB of HBM per device.

```python
import math
import jax
import jax.numpy as jnp
import numpy as np
from jax import lax

COLUMNS = 512
ROWS_DEV = 1024
PICKS_PER = 4
CAPACITY = 16
SKETCH_ROWS = 1024
PANEL_ROWS = 32768
N_GRP = 4
N_DEV = 8


def draw_panel(key, part):
    row_key = jax.random.fold_in(key, 11)
    col_key = jax.random.fold_in(key, 12)
    base_key = jax.random.fold_in(key, 13)
    row_scale = 0.3 * jnp.exp(jax.random.uniform(row_key, (PANEL_ROWS, 1), minval=0.0, maxval=math.log(10.0)))
    col_scale = 0.3 * jnp.exp(jax.random.uniform(col_key, (1, COLUMNS), minval=0.0, maxval=math.log(10.0)))
    base = jnp.clip(jax.random.normal(base_key, (PANEL_ROWS, COLUMNS)), -5.0, 5.0)
    values = base * row_scale * col_scale
    return values.astype(jnp.float32)


def draw_source_row(key, part):
    band_size = ROWS_DEV // N_DEV
    width = N_DEV * PICKS_PER
    offset_key = jax.random.fold_in(key, 21)
    offset = jax.random.randint(offset_key, (N_GRP, N_DEV, width), 0, band_size)
    flat_place = jnp.arange(N_GRP * N_DEV * width, dtype=jnp.int32).reshape(N_GRP, N_DEV, width)
    offset = jnp.where(flat_place == 0, 0, offset)
    offset = jnp.where(flat_place == N_GRP * N_DEV * width - 1, band_size - 1, offset)
    band = jnp.arange(width, dtype=jnp.int32) // PICKS_PER * band_size
    return (band[None, None, :] + offset).astype(jnp.int32)


def set_ends(values, key, least, largest):
    spot = [jax.random.randint(jax.random.fold_in(key, axis), (), 0, length) for axis, length in enumerate(values.shape)]
    main_axis = values.shape.index(max(values.shape))
    beside = spot[:main_axis] + [(spot[main_axis] + 1) % values.shape[main_axis]] + spot[main_axis + 1:]
    return values.at[tuple(spot)].set(least).at[tuple(beside)].set(largest)


def deal_out(rng, own, number, rows, number_of, top, reach, skew):
    sequence = jax.random.permutation(rng, number_of)
    packed, usual = shares(number_of, rows * top, reach, skew, True), shares(number_of, rows * top, reach, skew, False)
    places = jnp.arange(number_of)

    def named(sizes, rotation):
        used = int((sizes > 0).sum())
        fixed = max(1, used // 4)
        shifted = fixed + (places - fixed + rotation * (used - fixed)) % max(1, number_of - fixed)
        return jnp.zeros((number_of,), jnp.int32).at[sequence[jnp.where(places < fixed, places, shifted)]].set(jnp.asarray(sizes, jnp.int32))

    sizes = jnp.where(number % 4 == 0, named(packed, number // 4), named(usual, number - number // 4 - 1))
    mixed = jax.random.permutation(jax.random.fold_in(own, 3), number_of)
    donor, receiver = mixed[0:number_of // 2 * 2:2], mixed[1:number_of // 2 * 2:2]
    slack = jnp.minimum(sizes[donor] - 1, reach - sizes[receiver]) // 2
    slack = jnp.where((donor == sequence[0]) | (receiver == sequence[0]) | (sizes[receiver] == 0), 0, jnp.maximum(slack, 0))
    shifted = jax.random.randint(jax.random.fold_in(own, 4), (number_of // 2,), 0, 1 << 20) % (slack + 1)
    sizes = sizes.at[donor].add(-shifted).at[receiver].add(shifted)
    items = jnp.searchsorted(jnp.cumsum(sizes), jnp.arange(rows * top), side="right").astype(jnp.int32)
    table = items.reshape(top, rows).T
    table = table[jax.random.permutation(jax.random.fold_in(own, 1), rows)]
    rotation = jax.random.randint(jax.random.fold_in(own, 2), (rows, 1), 0, top)
    return jnp.take_along_axis(table, (jnp.arange(top)[None, :] + rotation) % top, axis=1)


def shares(amount, total, most, lean, full):
    portions = [(1 << 20) // math.isqrt(grade ** lean) + 1 for grade in range(1, amount + 1)]
    largest = most if full else min(most, max(-(-total // amount), total * portions[0] // sum(portions)))
    least = 1 if total - largest >= amount - 1 else 0
    counts, rest = [largest] + [least] * (amount - 1), total - largest - least * (amount - 1)
    while rest > 0:
        candidates = [i for i in range(1, amount) if counts[i] < largest] or [i for i in range(1, amount) if counts[i] < most]
        pool, remaining = sum([portions[i] for i in candidates]), rest
        for i in candidates:
            extra = min(most - counts[i], max(1, remaining * portions[i] // pool), rest)
            counts[i] = counts[i] + extra
            rest = rest - extra
    return np.array(counts)


def setup_inputs(seed: int = 0) -> dict:
    splits = jax.random.split(jax.random.key(seed), 5)
    panel = draw_panel(jax.random.fold_in(splits[4], 71), 0)
    signs = set_ends(jax.random.randint(splits[1], (PANEL_ROWS,), 0, 2), jax.random.fold_in(splits[1], 1), 0, 1).astype(jnp.int32)
    source_group_keys = jax.random.split(jax.random.fold_in(splits[2], 1), N_GRP * N_DEV * (N_DEV * PICKS_PER) // (N_DEV * PICKS_PER))
    source_group_turns = jax.random.permutation(jax.random.fold_in(splits[2], 3), N_GRP * N_DEV * (N_DEV * PICKS_PER) // (N_DEV * PICKS_PER))
    source_group = jax.vmap(lambda own, number: deal_out(jax.random.fold_in(splits[2], 2), own, number, N_DEV * PICKS_PER, N_GRP, 1, CAPACITY, 2))(source_group_keys, source_group_turns).reshape((N_GRP, N_DEV, N_DEV * PICKS_PER, 1))
    source_row = draw_source_row(jax.random.fold_in(splits[4], 71), 0)
    return {"panel": panel, "signs": signs, "source_group": source_group, "source_row": source_row}


def bit_parity(value, bits):
    total = jnp.zeros_like(value)
    for bit_place in range(bits):
        total = total + (value >> bit_place & 1)
    return total & 1

def walsh(block):
    order = block.shape[0]
    result = block
    span = 1
    for level in range(int(math.log2(order))):
        shaped = result.reshape(order // (2 * span), 2, span, -1)
        upper = shaped[:, 0]
        below = shaped[:, 1]
        result = jnp.stack([upper + below, upper - below], axis=1).reshape(order, -1)
        span = span * 2
    return result

def reference(panel, signs, source_group, source_row):
    flipped = panel * (1 - 2 * signs).astype(jnp.float32)[:, None]
    inner = lax.map(walsh, flipped.reshape(N_GRP, N_DEV * ROWS_DEV, COLUMNS))
    column = jnp.arange(N_DEV, dtype=jnp.int32)[None, :, None]
    position = (column * ROWS_DEV + source_row).astype(jnp.int32)
    picked_group = source_group[..., 0]
    total = jnp.zeros((N_GRP, N_DEV, N_DEV * PICKS_PER, COLUMNS), jnp.float32)
    for other in range(N_GRP):
        parity = bit_parity(picked_group & other, N_GRP.bit_length())
        factor = (1 - 2 * parity).astype(jnp.float32)
        total = total + factor[..., None] * inner[other][position]
    sampled = total * (1.0 / math.sqrt(PANEL_ROWS))
    sketch = sampled.reshape(N_GRP, N_DEV, N_DEV, PICKS_PER, COLUMNS).transpose(0, 2, 1, 3, 4).reshape(SKETCH_ROWS, COLUMNS)
    gram = jnp.dot(sketch.T.astype(jnp.float32), sketch.astype(jnp.float32), precision=lax.Precision.HIGHEST, preferred_element_type=jnp.float32) / SKETCH_ROWS
    gram = gram + 0.001 * jnp.eye(COLUMNS, dtype=jnp.float32)
    lower = jnp.linalg.cholesky(gram)
    conditioned = lax.linalg.triangular_solve(lower, panel, left_side=False, lower=True, transpose_a=True)
    return (sketch, conditioned)
```

```python
import functools
import math
import jax
import jax.numpy as jnp
from jax import lax
from jax.experimental import pallas as pl
from jax.experimental.pallas import tpu as pltpu
from jax.sharding import PartitionSpec as P

BLOCK = 128


def pivot_block(tiles):
    count = len(tiles)
    lane = lax.broadcasted_iota(jnp.int32, (8, BLOCK), 1)
    sub = lax.broadcasted_iota(jnp.int32, (8, BLOCK), 0)
    tiles = list(tiles)
    for p in range(count):
        base = 8 * p
        inside = (lane >= base) & (lane < base + 8)
        cols = {
            q: [jnp.broadcast_to(tiles[q][:, base + t : base + t + 1], (8, BLOCK)) for t in range(8)]
            for q in range(p, count)
        }
        tiles[p] = jnp.where(inside, (lane - base == sub).astype(jnp.float32), tiles[p])
        for q in range(p + 1, count):
            tiles[q] = jnp.where(inside, 0.0, tiles[q])
        diag = jnp.ones((8, BLOCK), jnp.float32)
        for t in range(8):
            pivot = jnp.broadcast_to(cols[p][t][t : t + 1, :], (8, BLOCK))
            diag = jnp.where(sub == t, pivot, diag)
            inverse = 1.0 / pivot
            row = jnp.broadcast_to(tiles[p][t : t + 1, :], (8, BLOCK)) * inverse
            heads = [
                jnp.broadcast_to(cols[p][u][t : t + 1, :], (8, BLOCK)) * inverse for u in range(t + 1, 8)
            ]
            for q in range(p, count):
                coef = cols[q][t]
                if q == p:
                    coef = jnp.where(sub > t, coef, 0.0)
                for place, u in enumerate(range(t + 1, 8)):
                    cols[q][u] = cols[q][u] - coef * heads[place]
                tiles[q] = tiles[q] - coef * row
        tiles[p] = tiles[p] * lax.rsqrt(diag)
    return tiles


def inverse_factor(work):
    size = work.shape[0]
    rowi = lax.broadcasted_iota(jnp.int32, (BLOCK, BLOCK), 0)
    coli = lax.broadcasted_iota(jnp.int32, (BLOCK, BLOCK), 1)
    wide = lax.broadcasted_iota(jnp.int32, (BLOCK, size), 1)

    def step(k, carry):
        start = pl.multiple_of(k * BLOCK, BLOCK)
        here = pl.ds(start, BLOCK)
        tiles = [
            work[pl.ds(pl.multiple_of(start + 8 * p, 8), 8), here] for p in range(BLOCK // 8)
        ]
        tiles = pivot_block(tiles)
        own = jnp.where(rowi >= coli, jnp.concatenate(tiles, axis=0), 0.0)
        rows = split_matmul(halves(own), halves(work[here, :]), ((1,), (0,)))
        work[here, :] = rows
        work[here, here] = own
        rows = work[here, :]

        @pl.when(start + BLOCK < size)
        def _():
            work[:, here] = jnp.where(
                lax.broadcasted_iota(jnp.int32, (size, BLOCK), 0) >= start + BLOCK, 0.0, work[:, here]
            )
            left = jnp.where(wide >= start + BLOCK, rows, 0.0)
            work[...] = work[...] - split_matmul(halves(left), halves(rows), ((0,), (0,)))

        work[here, :] = jnp.where(wide < start + BLOCK, rows, 0.0)
        return carry

    lax.fori_loop(0, size // BLOCK, step, 0)


def add_ridge(gram, sketch_total):
    size = gram.shape[0]
    rowi = lax.broadcasted_iota(jnp.int32, (size, size), 0)
    coli = lax.broadcasted_iota(jnp.int32, (size, size), 1)
    return gram / sketch_total + jnp.where(rowi == coli, 0.001, 0.0)


def halves(value):
    high = value.astype(jnp.bfloat16)
    return high, (value - high.astype(jnp.float32)).astype(jnp.bfloat16)


def split_matmul(a, b, dims):
    dot = functools.partial(
        lax.dot_general, dimension_numbers=(dims, ((), ())), preferred_element_type=jnp.float32
    )
    return dot(a[0], b[0]) + (dot(a[0], b[1]) + dot(a[1], b[0]))


def finish(work, panel_ref, out_ref):
    rows, columns = panel_ref.shape
    part = columns // 2
    for base in (0, part):
        deep = base + part
        factor = halves(work[base : base + part, 0:deep])
        out_ref[:, base : base + part] = split_matmul(
            halves(panel_ref[:, 0:deep]), factor, ((1,), (1,))
        )


def from_gram_kernel(sketch_total, gram_ref, panel_ref, out_ref, work):
    work[...] = add_ridge(gram_ref[...], sketch_total)
    inverse_factor(work)
    finish(work, panel_ref, out_ref)


def flip(index, mask):
    bit = 1
    while bit <= mask:
        if mask & bit:
            index = index + bit - 2 * bit * lax.rem(lax.div(index, bit), 2)
        bit = 2 * bit
    return index


def parity_sign(value, bits):
    span = 1
    while span < bits:
        span = span * 2
    while span > 1:
        span = span // 2
        value = value ^ (value >> span)
    return (1 - 2 * (value & 1)).astype(jnp.float32)


def pivot_rows(block):
    size = block.shape[1]
    lane = lax.broadcasted_iota(jnp.int32, (8, size), 1)
    sub = lax.broadcasted_iota(jnp.int32, (8, size), 0)
    done = []
    for p in range(size // 8):
        base = 8 * p
        tile, below = block[0:8], block[8:]
        cols = [jnp.broadcast_to(tile[:, base + t : base + t + 1], (8, size)) for t in range(8)]
        entry = {
            (u, t): jnp.broadcast_to(cols[t][u : u + 1, :], (8, size)) for t in range(8) for u in range(t, 8)
        }
        tile = jnp.where((lane >= base) & (lane < base + 8), (lane - base == sub).astype(jnp.float32), tile)
        rows = [jnp.broadcast_to(tile[t : t + 1, :], (8, size)) for t in range(8)]
        inverse, ratio = [], {}
        for t in range(8):
            inverse.append(1.0 / entry[t, t])
            for u in range(t + 1, 8):
                ratio[u, t] = entry[u, t] * inverse[t]
            for u in range(t + 1, 8):
                for v in range(t + 1, u + 1):
                    entry[u, v] = entry[u, v] - ratio[u, t] * entry[v, t]
                rows[u] = rows[u] - ratio[u, t] * rows[t]
        own = jnp.zeros((8, size), jnp.float32)
        for t in range(8):
            own = jnp.where(sub == t, rows[t] * lax.rsqrt(entry[t, t]), own)
        done.append(own)
        if base + 8 == size:
            break
        solved = [rows[t] * inverse[t] for t in range(8)]
        for t in range(7, 0, -1):
            for s in range(t):
                solved[s] = solved[s] - ratio[t, s] * solved[t]
        count = below.shape[0]
        wide = lax.broadcasted_iota(jnp.int32, below.shape, 1)
        block = jnp.where((wide >= base) & (wide < base + 8), 0.0, below)
        for t in range(8):
            coef = jnp.broadcast_to(below[:, base + t : base + t + 1], below.shape)
            block = block - coef * jnp.concatenate([solved[t]] * (count // 8), axis=0)
    own = jnp.concatenate(done, axis=0)
    rowi = lax.broadcasted_iota(jnp.int32, (size, size), 0)
    coli = lax.broadcasted_iota(jnp.int32, (size, size), 1)
    return jnp.where(rowi >= coli, own, 0.0)


ODD, EVEN = (7, 3, 5, 1), (6, 2, 4, 0)
LISTS, SLOTS = 14, 26


def sketch_kernel(
    groups, per_owner, scale, sketch_total, panel_hbm, signs_ref, group_ref, row_ref, own_ref, high_ref, low_ref,
    panel_ref, lists, values, split, choice, tables, odd, even, from_core, from_first, from_second, from_group,
    whole, parts_high, parts_low, block, product, loaded, send, recv,
):
    devices = 8
    rows_here, columns = panel_ref.shape
    turns = columns // BLOCK
    band = groups * devices * per_owner
    share = devices * per_owner
    half = band // 2
    left, right = pl.ds(0, half), pl.ds(half, half)
    me = lax.axis_index("dev")
    here = lax.axis_index("grp")
    load = pltpu.make_async_copy(panel_hbm, panel_ref, loaded)
    load.start()

    barrier = pltpu.get_barrier_semaphore()
    for mask in range(1, devices):
        pl.semaphore_signal(
            barrier, inc=1, device_id={"dev": flip(me, mask)}, device_id_type=pl.DeviceIdType.MESH
        )
    for mask in range(1, groups):
        pl.semaphore_signal(
            barrier, inc=1, device_id={"grp": flip(here, mask)}, device_id_type=pl.DeviceIdType.MESH
        )
    pl.semaphore_wait(barrier, devices + groups - 2)

    def remote(source, target, place, axis, mask):
        peer = flip(me if axis == "dev" else here, mask)
        return functools.partial(
            pltpu.make_async_remote_copy,
            src_ref=source,
            dst_ref=target,
            send_sem=send.at[place],
            recv_sem=recv.at[place],
            device_id={axis: peer},
            device_id_type=pl.DeviceIdType.MESH,
        )

    listed = [
        remote(ref, lists.at[kind, mask], kind * 7 + mask - 1, "dev", mask)
        for mask in range(1, devices)
        for kind, ref in enumerate((group_ref, row_ref))
    ]
    for copy in listed:
        copy().start()
    load.wait()
    for turn in range(turns):
        now = panel_ref[:, turn * BLOCK : (turn + 1) * BLOCK]
        top, rest = halves(now)
        split[turn, :, 0:BLOCK] = top
        split[turn, :, BLOCK : 2 * BLOCK] = rest
    lists[0, 0] = group_ref[...]
    lists[1, 0] = row_ref[...]
    for copy in listed:
        copy().wait_recv()

    for slot in range(devices):
        values[slot * groups : (slot + 1) * groups, :] = (
            lists[0, slot] * devices + flip(me, slot)
        ) * rows_here + lists[1, slot]
    total = devices * band
    width = devices * per_owner
    place = lax.broadcasted_iota(jnp.int32, (total, width), 0)
    entry = lax.broadcasted_iota(jnp.int32, (total, width), 1)
    wanted = ((place // band) ^ me) * per_owner + place % per_owner
    spread = lax.dot_general(
        (entry == wanted).astype(jnp.float32),
        values[...].astype(jnp.float32),
        (((1,), (1,)), ((), ())),
        precision=lax.Precision.HIGHEST,
        preferred_element_type=jnp.float32,
    )
    place = lax.broadcasted_iota(jnp.int32, (total, devices * groups), 0)
    held = lax.broadcasted_iota(jnp.int32, (total, devices * groups), 1)
    source = (((place // per_owner) % devices) ^ me) * groups + (((place // share) % groups) ^ here)
    choice[...] = jnp.sum(jnp.where(held == source, spread, 0.0), axis=1, keepdims=True).astype(jnp.int32)

    def table(chunk):
        pick = jnp.broadcast_to(choice[chunk * band : (chunk + 1) * band, :], (band, 128))
        lane = lax.broadcasted_iota(jnp.int32, (band, 128), 1)
        rank = here * devices + me
        above = parity_sign((pick // rows_here) & rank, (groups * devices).bit_length() - 1)
        part = [parity_sign(pick & lane, 7) * above]
        bit = 7
        while 128 * len(part) < rows_here:
            turn = (1 - 2 * ((pick >> bit) & 1)).astype(jnp.float32)
            part = part + [one * turn for one in part]
            bit = bit + 1
        turned = (1 - 2 * signs_ref[...]).astype(jnp.float32)
        part = [(one * turned[i : i + 1, :]).astype(jnp.bfloat16) for i, one in enumerate(part)]
        return jnp.concatenate(part, axis=1)

    def mixed(side, turn):
        both = lax.dot_general(
            tables[side], split[turn], (((1,), (0,)), ((), ())), preferred_element_type=jnp.float32
        )
        return (both[:, 0:BLOCK] + both[:, BLOCK : 2 * BLOCK]).reshape(4, band, BLOCK)

    def at(turn, place):
        return LISTS + SLOTS * turn + place

    def core(t):
        return [remote(odd.at[t, i], from_core.at[t, i], at(t, i), "dev", 1) for i in range(4)]

    def first(t):
        return [
            remote(even.at[t, 0, left], from_first.at[t, 1, left], at(t, 4), "dev", 2),
            remote(even.at[t, 0, right], from_first.at[t, 1, right], at(t, 5), "dev", 4),
            remote(even.at[t, 1, left], from_first.at[t, 0, left], at(t, 6), "dev", 2),
            remote(even.at[t, 2, right], from_first.at[t, 0, right], at(t, 7), "dev", 4),
        ]

    def second(t):
        return [
            remote(even.at[t, 2, left], from_second.at[t, left], at(t, 8), "dev", 4),
            remote(even.at[t, 1, right], from_second.at[t, right], at(t, 9), "dev", 2),
        ]

    def gathered(t):
        return [
            remote(even.at[t, 3, pl.ds(b * share, share)], from_group.at[t, b], at(t, 9 + b), "grp", b)
            for b in range(1, groups)
        ]

    def shared(t):
        mine = whole.at[t, 0, pl.ds(0, share)]
        return [
            remote(mine, whole.at[t, 0, pl.ds(b * share, share)], at(t, 12 + b), "grp", b)
            for b in range(1, groups)
        ]

    def out(t):
        return [
            remote(whole.at[t, 0, left], whole.at[t, 4, left], at(t, 16), "dev", 4),
            remote(whole.at[t, 0, right], whole.at[t, 2, right], at(t, 17), "dev", 2),
            remote(whole.at[t, 0, left], whole.at[t, 2, left], at(t, 18), "dev", 2),
            remote(whole.at[t, 0, right], whole.at[t, 4, right], at(t, 19), "dev", 4),
        ]

    def relay(t):
        return [
            remote(whole.at[t, 4, left], whole.at[t, 6, left], at(t, 20), "dev", 2),
            remote(whole.at[t, 2, right], whole.at[t, 6, right], at(t, 21), "dev", 4),
        ]

    def hand(t):
        return [
            remote(whole.at[t, 2 * i], whole.at[t, 2 * i + 1], at(t, 22 + i), "dev", 1) for i in range(4)
        ]

    def step0(t):
        odd[t] = mixed(0, t)
        for copy in core(t):
            copy().start()

    def step1(t):
        even[t] = mixed(1, t)
        arrived, going = core(t), first(t)
        for i in range(4):
            arrived[i]().wait_recv()
            even[t, i] = even[t, i] + from_core[t, i]
            for copy in (going[0:2], going[2:3], going[3:4], ())[i]:
                copy().start()

    def step2(t):
        arrived, going = first(t), second(t)
        arrived[0]().wait_recv()
        even[t, 2, left] = even[t, 2, left] + from_first[t, 1, left]
        going[0]().start()
        arrived[1]().wait_recv()
        even[t, 1, right] = even[t, 1, right] + from_first[t, 1, right]
        going[1]().start()

    def step3(t):
        for copy in first(t)[2:4] + second(t):
            copy().wait_recv()
        even[t, 3] = even[t, 3] + from_first[t, 0] + from_second[t]
        for copy in gathered(t):
            copy().start()

    def step4(t):
        result = even[t, 3, pl.ds(0, share)]
        for b, copy in enumerate(gathered(t)):
            copy().wait_recv()
            result = result + from_group[t, b + 1]
        whole[t, 0, pl.ds(0, share)] = result * scale
        for copy in shared(t):
            copy().start()
        own_ref[:, t * BLOCK : (t + 1) * BLOCK] = result * scale

    def step5(t):
        for copy in shared(t):
            copy().wait_recv()
        for copy in out(t) + hand(t)[0:1]:
            copy().start()

    def step6(t):
        arrived, on, going = out(t), relay(t), hand(t)
        for i in range(2):
            arrived[i]().wait_recv()
            on[i]().start()
        for i in range(2):
            arrived[2 + i]().wait_recv()
            going[1 + i]().start()

    def step7(t):
        for copy in relay(t):
            copy().wait_recv()
        hand(t)[3]().start()

    def gram_step(k):
        here_k = slice(k * BLOCK, (k + 1) * BLOCK)
        deep = (k + 1) * BLOCK
        now = halves(whole[k].reshape(devices * band, BLOCK))
        parts_high[:, here_k] = now[0]
        parts_low[:, here_k] = now[1]
        gram = split_matmul(now, (parts_high[:, 0:deep], parts_low[:, 0:deep]), ((0,), (0,))) / sketch_total
        rowi = lax.broadcasted_iota(jnp.int32, (BLOCK, BLOCK), 0)
        coli = lax.broadcasted_iota(jnp.int32, (BLOCK, BLOCK), 1)
        corner = gram[:, here_k] + jnp.where(rowi == coli, 0.001, 0.0)
        if k > 0:
            before = k * BLOCK
            known = high_ref[0:before, 0:before], low_ref[0:before, 0:before]
            lower = halves(split_matmul(halves(gram[:, 0:before]), known, ((1,), (1,))))
            corner = corner - split_matmul(lower, lower, ((1,), (1,)))
            product[:, 0:before] = split_matmul(lower, known, ((1,), (0,)))
        block[...] = corner

    def row_step(k):
        here_k = slice(k * BLOCK, (k + 1) * BLOCK)
        own = halves(block[...])
        for target, part in zip((high_ref, low_ref), own):
            target[here_k, here_k] = part
            if k + 1 < turns:
                target[here_k, (k + 1) * BLOCK :] = jnp.zeros((BLOCK, columns - (k + 1) * BLOCK), jnp.bfloat16)
        if k > 0:
            before = k * BLOCK
            rows = halves(-split_matmul(own, halves(product[:, 0:before]), ((1,), (0,))))
            for target, part in zip((high_ref, low_ref), rows):
                target[here_k, 0:before] = part

    for side, chunks in enumerate((ODD, EVEN)):
        for i, chunk in enumerate(chunks):
            tables[side, i * band : (i + 1) * band, :] = table(chunk)
        if side == 0:
            step0(0)
    steps = (step0, step1, step2, step3, step4, step5, step6, step7)
    for tick in range(1, 8):
        for place in range(7, -1, -1):
            if 0 <= tick - place < turns:
                steps[place](tick - place)

    def factor(k, carry):
        for ahead, step in ((1, step7), (2, step6), (3, step5)):
            @pl.when(k + ahead < turns)
            def _(ahead=ahead, step=step):
                step(k + ahead)

        for copy in hand(k):
            copy().wait_recv()
        for place in range(turns):
            @pl.when(k == place)
            def _(place=place):
                gram_step(place)
        block[...] = pivot_rows(block[...])
        for place in range(turns):
            @pl.when(k == place)
            def _(place=place):
                row_step(place)
        return carry

    lax.fori_loop(0, turns, factor, 0)
    for copy in listed:
        copy().wait_send()

    def drain(t, carry):
        for copy in core(t) + first(t) + second(t) + gathered(t) + shared(t) + out(t) + relay(t) + hand(t):
            copy().wait_send()
        return carry

    lax.fori_loop(0, turns, drain, 0)


def kernel_sketch(panel, signs, source_group, source_row, groups, devices):
    rows_here, columns = panel.shape
    per_owner = source_row.shape[2] // devices
    band = groups * devices * per_owner
    share = devices * per_owner
    turns = columns // BLOCK
    scale = 1.0 / math.sqrt(rows_here * devices * groups)
    vmem = pl.BlockSpec(memory_space=pltpu.VMEM)
    f32, bf16 = jnp.float32, jnp.bfloat16
    places = LISTS + SLOTS * turns
    return pl.pallas_call(
        functools.partial(sketch_kernel, groups, per_owner, scale, devices * band),
        out_shape=[
            jax.ShapeDtypeStruct((share, columns), f32),
            jax.ShapeDtypeStruct((columns, columns), bf16),
            jax.ShapeDtypeStruct((columns, columns), bf16),
        ],
        in_specs=[pl.BlockSpec(memory_space=pl.ANY)] + [vmem] * 3,
        out_specs=[vmem] * 3,
        scratch_shapes=[
            pltpu.VMEM((rows_here, columns), f32),
            pltpu.VMEM((2, devices, groups, share), jnp.int32),
            pltpu.VMEM((devices * groups, share), jnp.int32),
            pltpu.VMEM((turns, rows_here, 2 * BLOCK), bf16),
            pltpu.VMEM((devices * band, 1), jnp.int32),
            pltpu.VMEM((2, 4 * band, rows_here), bf16),
            pltpu.VMEM((turns, 4, band, BLOCK), f32),
            pltpu.VMEM((turns, 4, band, BLOCK), f32),
            pltpu.VMEM((turns, 4, band, BLOCK), f32),
            pltpu.VMEM((turns, 2, band, BLOCK), f32),
            pltpu.VMEM((turns, band, BLOCK), f32),
            pltpu.VMEM((turns, groups, share, BLOCK), f32),
            pltpu.VMEM((turns, devices, band, BLOCK), f32),
            pltpu.VMEM((devices * band, columns), bf16),
            pltpu.VMEM((devices * band, columns), bf16),
            pltpu.VMEM((BLOCK, BLOCK), f32),
            pltpu.VMEM((BLOCK, columns), f32),
            pltpu.SemaphoreType.DMA,
            pltpu.SemaphoreType.DMA((places,)),
            pltpu.SemaphoreType.DMA((places,)),
        ],
        compiler_params=pltpu.CompilerParams(collective_id=0, has_side_effects=True),
        name="sketch",
    )(
        panel,
        signs.reshape(rows_here // 128, 128),
        source_group.reshape(groups, share),
        source_row.reshape(groups, share),
    )


def apply_kernel(sketch_ref, high_ref, low_ref, panel_ref, own_ref, out_ref):
    @pl.when(pl.program_id(0) == 0)
    def _():
        own_ref[...] = sketch_ref[...]

    columns = panel_ref.shape[1]
    part = columns // 2
    panel = halves(panel_ref[...])
    for base in (0, part):
        deep = base + part
        factor = high_ref[base:deep, 0:deep], low_ref[base:deep, 0:deep]
        out_ref[:, base:deep] = split_matmul((panel[0][:, 0:deep], panel[1][:, 0:deep]), factor, ((1,), (1,)))


def apply_factor(sketch, high, low, panel):
    rows_here, columns = panel.shape
    part = 256
    fixed = lambda i: (0, 0)
    moving = pl.BlockSpec((part, columns), lambda i: (i, 0))
    once = pl.Buffered(1)
    return pl.pallas_call(
        apply_kernel,
        grid=(rows_here // part,),
        out_shape=[
            jax.ShapeDtypeStruct(sketch.shape, jnp.float32),
            jax.ShapeDtypeStruct(panel.shape, jnp.float32),
        ],
        in_specs=[
            pl.BlockSpec(sketch.shape, fixed, pipeline_mode=once),
            pl.BlockSpec(high.shape, fixed, pipeline_mode=once),
            pl.BlockSpec(low.shape, fixed, pipeline_mode=once),
            moving,
        ],
        out_specs=[pl.BlockSpec(sketch.shape, fixed), moving],
        name="apply",
    )(sketch, high, low, panel)


def bit_parity(value, bits):
    total = jnp.zeros_like(value)
    for bit_place in range(bits):
        total = total + (value >> bit_place & 1)
    return total & 1


def sylvester(order):
    index = jnp.arange(order, dtype=jnp.int32)
    parity = bit_parity(index[:, None] & index[None, :], order.bit_length())
    return (1 - 2 * parity).astype(jnp.float32)


def general_sketch(panel, signs, source_group, source_row):
    rows_here = panel.shape[0]
    columns = panel.shape[1]
    groups = lax.axis_size("grp")
    devices = lax.axis_size("dev")
    group_here = lax.axis_index("grp")
    highest = lax.Precision.HIGHEST
    flipped = panel * (1 - 2 * signs).astype(jnp.float32)[:, None]
    local = jnp.dot(
        sylvester(rows_here), flipped, precision=highest, preferred_element_type=jnp.float32
    )
    dev_table = sylvester(devices)
    mixed = jnp.einsum(
        "ed,dbc->ebc",
        dev_table,
        lax.all_to_all(
            local.reshape(devices, rows_here // devices, columns),
            "dev",
            split_axis=0,
            concat_axis=0,
            tiled=True,
        ),
        precision=highest,
    )
    inner = mixed
    inner = inner.reshape(rows_here, columns)
    chosen_group = source_group[:, 0, :, 0]
    chosen_row = source_row[:, 0, :]
    width = chosen_group.shape[1]
    per_owner = width // devices
    band_size = rows_here // devices
    dev_here = lax.axis_index("dev")
    stacked = jnp.stack([chosen_group, chosen_row]).reshape(2, groups, devices, per_owner)
    lists = lax.all_to_all(stacked, "dev", split_axis=2, concat_axis=2, tiled=True)
    band_group = lists[0].reshape(-1)
    band_row = lists[1].reshape(-1)
    flat_place = jnp.arange(groups * devices * per_owner, dtype=jnp.int32)
    source_dev = flat_place // per_owner % devices
    flat_index = source_dev * band_size + band_row - dev_here * band_size
    parity = bit_parity(band_group & group_here, groups.bit_length())
    factor = (1 - 2 * parity).astype(jnp.float32)
    gathered = lax.psum_scatter(
        inner[flat_index] * factor[:, None], "grp", scatter_dimension=0, tiled=True
    )
    panel_total = rows_here * devices * groups
    sketch = gathered * (1.0 / math.sqrt(panel_total))
    sketch_total = sketch.shape[0] * devices * groups
    partial_gram = jnp.dot(sketch.T, sketch, precision=highest, preferred_element_type=jnp.float32)
    return sketch, lax.psum(partial_gram, ("grp", "dev"))


def on_device(panel, signs, source_group, source_row):
    rows_here, columns = panel.shape
    groups = lax.axis_size("grp")
    devices = lax.axis_size("dev")
    width = source_row.shape[2]
    sketch_total = groups * devices * width
    fits = groups == 4 and devices == 8 and groups * width == BLOCK
    if fits and columns == 4 * BLOCK and rows_here % 256 == 0 and rows_here & (rows_here - 1) == 0:
        sketch, high, low = kernel_sketch(panel, signs, source_group, source_row, groups, devices)
        sketch, conditioned = apply_factor(sketch, high, low, panel)
        return (sketch, conditioned)
    sketch, gram = general_sketch(panel, signs, source_group, source_row)
    conditioned = pl.pallas_call(
        functools.partial(from_gram_kernel, sketch_total),
        out_shape=jax.ShapeDtypeStruct((rows_here, columns), jnp.float32),
        in_specs=[pl.BlockSpec(memory_space=pltpu.VMEM)] * 2,
        out_specs=pl.BlockSpec(memory_space=pltpu.VMEM),
        scratch_shapes=[pltpu.VMEM((columns, columns), jnp.float32)],
        name="factor",
    )(gram, panel)
    return (sketch, conditioned)


def solution(mesh):
    return jax.shard_map(
        on_device,
        mesh=mesh,
        in_specs=(
            P(("grp", "dev"), None),
            P(("grp", "dev")),
            P(None, "dev", None, None),
            P(None, "dev", None),
        ),
        out_specs=(P(("grp", "dev"), None), P(("grp", "dev"), None)),
        check_vma=False,
    )
```

```python
import functools
import math
import jax
import jax.numpy as jnp
from jax import lax
from jax.experimental import pallas as pl
from jax.experimental.pallas import tpu as pltpu
from jax.sharding import PartitionSpec as P

BLOCK = 128


def pivot_block(tiles):
    count = len(tiles)
    lane = lax.broadcasted_iota(jnp.int32, (8, BLOCK), 1)
    sub = lax.broadcasted_iota(jnp.int32, (8, BLOCK), 0)
    tiles = list(tiles)
    for p in range(count):
        base = 8 * p
        inside = (lane >= base) & (lane < base + 8)
        cols = {
            q: [jnp.broadcast_to(tiles[q][:, base + t : base + t + 1], (8, BLOCK)) for t in range(8)]
            for q in range(p, count)
        }
        tiles[p] = jnp.where(inside, (lane - base == sub).astype(jnp.float32), tiles[p])
        for q in range(p + 1, count):
            tiles[q] = jnp.where(inside, 0.0, tiles[q])
        diag = jnp.ones((8, BLOCK), jnp.float32)
        for t in range(8):
            pivot = jnp.broadcast_to(cols[p][t][t : t + 1, :], (8, BLOCK))
            diag = jnp.where(sub == t, pivot, diag)
            inverse = 1.0 / pivot
            row = jnp.broadcast_to(tiles[p][t : t + 1, :], (8, BLOCK)) * inverse
            heads = [
                jnp.broadcast_to(cols[p][u][t : t + 1, :], (8, BLOCK)) * inverse for u in range(t + 1, 8)
            ]
            for q in range(p, count):
                coef = cols[q][t]
                if q == p:
                    coef = jnp.where(sub > t, coef, 0.0)
                for place, u in enumerate(range(t + 1, 8)):
                    cols[q][u] = cols[q][u] - coef * heads[place]
                tiles[q] = tiles[q] - coef * row
        tiles[p] = tiles[p] * lax.rsqrt(diag)
    return tiles


def inverse_factor(work):
    size = work.shape[0]
    rowi = lax.broadcasted_iota(jnp.int32, (BLOCK, BLOCK), 0)
    coli = lax.broadcasted_iota(jnp.int32, (BLOCK, BLOCK), 1)
    wide = lax.broadcasted_iota(jnp.int32, (BLOCK, size), 1)

    def step(k, carry):
        start = pl.multiple_of(k * BLOCK, BLOCK)
        here = pl.ds(start, BLOCK)
        tiles = [
            work[pl.ds(pl.multiple_of(start + 8 * p, 8), 8), here] for p in range(BLOCK // 8)
        ]
        tiles = pivot_block(tiles)
        own = jnp.where(rowi >= coli, jnp.concatenate(tiles, axis=0), 0.0)
        rows = split_matmul(halves(own), halves(work[here, :]), ((1,), (0,)))
        work[here, :] = rows
        work[here, here] = own
        rows = work[here, :]

        @pl.when(start + BLOCK < size)
        def _():
            work[:, here] = jnp.where(
                lax.broadcasted_iota(jnp.int32, (size, BLOCK), 0) >= start + BLOCK, 0.0, work[:, here]
            )
            left = jnp.where(wide >= start + BLOCK, rows, 0.0)
            work[...] = work[...] - split_matmul(halves(left), halves(rows), ((0,), (0,)))

        work[here, :] = jnp.where(wide < start + BLOCK, rows, 0.0)
        return carry

    lax.fori_loop(0, size // BLOCK, step, 0)


def add_ridge(gram, sketch_total):
    size = gram.shape[0]
    rowi = lax.broadcasted_iota(jnp.int32, (size, size), 0)
    coli = lax.broadcasted_iota(jnp.int32, (size, size), 1)
    return gram / sketch_total + jnp.where(rowi == coli, 0.001, 0.0)


def halves(value):
    high = value.astype(jnp.bfloat16)
    return high, (value - high.astype(jnp.float32)).astype(jnp.bfloat16)


def split_matmul(a, b, dims):
    dot = functools.partial(
        lax.dot_general, dimension_numbers=(dims, ((), ())), preferred_element_type=jnp.float32
    )
    return dot(a[0], b[0]) + (dot(a[0], b[1]) + dot(a[1], b[0]))


def finish(work, panel_ref, out_ref):
    rows, columns = panel_ref.shape
    part = columns // 2
    for base in (0, part):
        deep = base + part
        factor = halves(work[base : base + part, 0:deep])
        out_ref[:, base : base + part] = split_matmul(
            halves(panel_ref[:, 0:deep]), factor, ((1,), (1,))
        )


def from_gram_kernel(sketch_total, gram_ref, panel_ref, out_ref, work):
    work[...] = add_ridge(gram_ref[...], sketch_total)
    inverse_factor(work)
    finish(work, panel_ref, out_ref)


def flip(index, mask):
    bit = 1
    while bit <= mask:
        if mask & bit:
            index = index + bit - 2 * bit * lax.rem(lax.div(index, bit), 2)
        bit = 2 * bit
    return index


def parity_sign(value, bits):
    span = 1
    while span < bits:
        span = span * 2
    while span > 1:
        span = span // 2
        value = value ^ (value >> span)
    return (1 - 2 * (value & 1)).astype(jnp.float32)


ODD, EVEN = (7, 3, 5, 1), (6, 2, 4, 0)
LISTS, SLOTS, MIDDLE = 14, 20, 9


def pivot_rows(block, halfway):
    size = block.shape[1]
    lane = lax.broadcasted_iota(jnp.int32, (8, size), 1)
    sub = lax.broadcasted_iota(jnp.int32, (8, size), 0)
    done = []
    for p in range(size // 8):
        base = 8 * p
        if p == MIDDLE:
            halfway()
        tile, below = block[0:8], block[8:]
        cols = [jnp.broadcast_to(tile[:, base + t : base + t + 1], (8, size)) for t in range(8)]
        entry = {
            (u, t): jnp.broadcast_to(cols[t][u : u + 1, :], (8, size)) for t in range(8) for u in range(t, 8)
        }
        tile = jnp.where((lane >= base) & (lane < base + 8), (lane - base == sub).astype(jnp.float32), tile)
        rows = [jnp.broadcast_to(tile[t : t + 1, :], (8, size)) for t in range(8)]
        inverse, ratio = [], {}
        for t in range(8):
            inverse.append(1.0 / entry[t, t])
            for u in range(t + 1, 8):
                ratio[u, t] = entry[u, t] * inverse[t]
            for u in range(t + 1, 8):
                for v in range(t + 1, u + 1):
                    entry[u, v] = entry[u, v] - ratio[u, t] * entry[v, t]
                rows[u] = rows[u] - ratio[u, t] * rows[t]
        own = jnp.zeros((8, size), jnp.float32)
        for t in range(8):
            own = jnp.where(sub == t, rows[t] * lax.rsqrt(entry[t, t]), own)
        done.append(own)
        if base + 8 == size:
            break
        solved = [rows[t] * inverse[t] for t in range(8)]
        for t in range(7, 0, -1):
            for s in range(t):
                solved[s] = solved[s] - ratio[t, s] * solved[t]
        count = below.shape[0]
        wide = lax.broadcasted_iota(jnp.int32, below.shape, 1)
        block = jnp.where((wide >= base) & (wide < base + 8), 0.0, below)
        for t in range(8):
            coef = jnp.broadcast_to(below[:, base + t : base + t + 1], below.shape)
            block = block - coef * jnp.concatenate([solved[t]] * (count // 8), axis=0)
    own = jnp.concatenate(done, axis=0)
    rowi = lax.broadcasted_iota(jnp.int32, (size, size), 0)
    coli = lax.broadcasted_iota(jnp.int32, (size, size), 1)
    return jnp.where(rowi >= coli, own, 0.0)


def sketch_kernel(
    groups, per_owner, scale, sketch_total, panel_hbm, signs_ref, group_ref, row_ref, own_ref, high_ref, low_ref,
    panel_ref, lists, values, split, choice, tables, odd, even, from_core, from_first, from_group,
    whole, parts_high, parts_low, block, product, loaded, send, recv,
):
    devices = 8
    rows_here, columns = panel_ref.shape
    turns = columns // BLOCK
    band = groups * devices * per_owner
    share = devices * per_owner
    me = lax.axis_index("dev")
    here = lax.axis_index("grp")
    load = pltpu.make_async_copy(panel_hbm, panel_ref, loaded)
    load.start()

    barrier = pltpu.get_barrier_semaphore()
    for mask in range(1, devices):
        pl.semaphore_signal(
            barrier, inc=1, device_id={"dev": flip(me, mask)}, device_id_type=pl.DeviceIdType.MESH
        )
    for mask in range(1, groups):
        pl.semaphore_signal(
            barrier, inc=1, device_id={"grp": flip(here, mask)}, device_id_type=pl.DeviceIdType.MESH
        )
    pl.semaphore_wait(barrier, devices + groups - 2)

    def remote(source, target, place, axis, mask):
        peer = flip(me if axis == "dev" else here, mask)
        return functools.partial(
            pltpu.make_async_remote_copy,
            src_ref=source,
            dst_ref=target,
            send_sem=send.at[place],
            recv_sem=recv.at[place],
            device_id={axis: peer},
            device_id_type=pl.DeviceIdType.MESH,
        )

    listed = [
        remote(ref, lists.at[kind, mask], kind * 7 + mask - 1, "dev", mask)
        for mask in range(1, devices)
        for kind, ref in enumerate((group_ref, row_ref))
    ]
    for copy in listed:
        copy().start()
    load.wait()
    for turn in range(turns):
        now = panel_ref[:, turn * BLOCK : (turn + 1) * BLOCK]
        top, rest = halves(now)
        split[turn, :, 0:BLOCK] = top
        split[turn, :, BLOCK : 2 * BLOCK] = rest
    lists[0, 0] = group_ref[...]
    lists[1, 0] = row_ref[...]
    for copy in listed:
        copy().wait_recv()

    for slot in range(devices):
        values[slot * groups : (slot + 1) * groups, :] = (
            lists[0, slot] * devices + flip(me, slot)
        ) * rows_here + lists[1, slot]
    total = devices * band
    width = devices * per_owner
    place = lax.broadcasted_iota(jnp.int32, (total, width), 0)
    entry = lax.broadcasted_iota(jnp.int32, (total, width), 1)
    wanted = ((place // band) ^ me) * per_owner + place % per_owner
    spread = lax.dot_general(
        (entry == wanted).astype(jnp.float32),
        values[...].astype(jnp.float32),
        (((1,), (1,)), ((), ())),
        precision=lax.Precision.HIGHEST,
        preferred_element_type=jnp.float32,
    )
    place = lax.broadcasted_iota(jnp.int32, (total, devices * groups), 0)
    held = lax.broadcasted_iota(jnp.int32, (total, devices * groups), 1)
    source = (((place // per_owner) % devices) ^ me) * groups + (((place // share) % groups) ^ here)
    choice[...] = jnp.sum(jnp.where(held == source, spread, 0.0), axis=1, keepdims=True).astype(jnp.int32)

    def table(chunk):
        pick = jnp.broadcast_to(choice[chunk * band : (chunk + 1) * band, :], (band, 128))
        lane = lax.broadcasted_iota(jnp.int32, (band, 128), 1)
        rank = here * devices + me
        above = parity_sign((pick // rows_here) & rank, (groups * devices).bit_length() - 1)
        part = [parity_sign(pick & lane, 7) * above]
        bit = 7
        while 128 * len(part) < rows_here:
            turn = (1 - 2 * ((pick >> bit) & 1)).astype(jnp.float32)
            part = part + [one * turn for one in part]
            bit = bit + 1
        turned = (1 - 2 * signs_ref[...]).astype(jnp.float32)
        part = [(one * turned[i : i + 1, :]).astype(jnp.bfloat16) for i, one in enumerate(part)]
        return jnp.concatenate(part, axis=1)

    def mixed(side, turn):
        both = lax.dot_general(
            tables[side], split[turn], (((1,), (0,)), ((), ())), preferred_element_type=jnp.float32
        )
        return (both[:, 0:BLOCK] + both[:, BLOCK : 2 * BLOCK]).reshape(4, band, BLOCK)

    def at(turn, place):
        return LISTS + SLOTS * turn + place

    def core(t):
        return [remote(odd.at[t, i], from_core.at[t, i], at(t, i), "dev", 1) for i in range(4)]

    def first(t):
        return [
            remote(even.at[t, i], from_first.at[t, i], at(t, 4 + i), "dev", mask)
            for i, mask in enumerate(EVEN[0:3])
        ]

    def gathered(t):
        return [
            remote(even.at[t, 3, pl.ds(b * share, share)], from_group.at[t, b], at(t, 6 + b), "grp", b)
            for b in (3, 2, 1)
        ]

    def shared(t):
        mine = whole.at[t, 0, pl.ds(0, share)]
        return [
            remote(mine, whole.at[t, 0, pl.ds(b * share, share)], at(t, 9 + b), "grp", b)
            for b in (3, 2, 1)
        ]

    def out(t):
        return [
            remote(whole.at[t, 0], whole.at[t, mask], at(t, 13 + i), "dev", mask)
            for i, mask in enumerate(EVEN[0:3])
        ]

    def hand(t):
        return [
            remote(whole.at[t, mask], whole.at[t, mask + 1], at(t, 16 + i), "dev", 1)
            for i, mask in enumerate(EVEN)
        ]

    def start_core(t):
        odd[t] = mixed(0, t)
        for copy in core(t):
            copy().start()

    def start_first(t):
        arrived, going = core(t), first(t)
        even[t] = mixed(1, t)
        for i in range(4):
            arrived[i]().wait_recv()
            even[t, i] = even[t, i] + from_core[t, i]
            if i < 3:
                going[i]().start()

    def start_gather(t):
        for copy in first(t):
            copy().wait_recv()
        even[t, 3] = even[t, 3] + from_first[t, 0] + (from_first[t, 1] + from_first[t, 2])
        for copy in gathered(t):
            copy().start()

    def start_share(t):
        for copy in gathered(t):
            copy().wait_recv()
        result = even[t, 3, pl.ds(0, share)] + from_group[t, 1] + (from_group[t, 2] + from_group[t, 3])
        whole[t, 0, pl.ds(0, share)] = result * scale
        for copy in shared(t):
            copy().start()
        own_ref[:, t * BLOCK : (t + 1) * BLOCK] = result * scale

    def start_out(t):
        for copy in shared(t):
            copy().wait_recv()
        for copy in out(t) + hand(t)[3:4]:
            copy().start()

    def start_hand(t):
        for copy, on in zip(out(t), hand(t)):
            copy().wait_recv()
            on().start()

    def gram_step(k):
        here_k = slice(k * BLOCK, (k + 1) * BLOCK)
        deep = (k + 1) * BLOCK
        now = halves(whole[k].reshape(devices * band, BLOCK))
        parts_high[:, here_k] = now[0]
        parts_low[:, here_k] = now[1]
        gram = split_matmul(now, (parts_high[:, 0:deep], parts_low[:, 0:deep]), ((0,), (0,))) / sketch_total
        rowi = lax.broadcasted_iota(jnp.int32, (BLOCK, BLOCK), 0)
        coli = lax.broadcasted_iota(jnp.int32, (BLOCK, BLOCK), 1)
        corner = gram[:, here_k] + jnp.where(rowi == coli, 0.001, 0.0)
        if k > 0:
            before = k * BLOCK
            known = high_ref[0:before, 0:before], low_ref[0:before, 0:before]
            lower = halves(split_matmul(halves(gram[:, 0:before]), known, ((1,), (1,))))
            corner = corner - split_matmul(lower, lower, ((1,), (1,)))
            product[:, 0:before] = split_matmul(lower, known, ((1,), (0,)))
        block[...] = corner

    def row_step(k):
        here_k = slice(k * BLOCK, (k + 1) * BLOCK)
        own = halves(block[...])
        for target, part in zip((high_ref, low_ref), own):
            target[here_k, here_k] = part
            if k + 1 < turns:
                target[here_k, (k + 1) * BLOCK :] = jnp.zeros((BLOCK, columns - (k + 1) * BLOCK), jnp.bfloat16)
        if k > 0:
            before = k * BLOCK
            rows = halves(-split_matmul(own, halves(product[:, 0:before]), ((1,), (0,))))
            for target, part in zip((high_ref, low_ref), rows):
                target[here_k, 0:before] = part

    for side, chunks in enumerate((ODD, EVEN)):
        for i, chunk in enumerate(chunks):
            tables[side, i * band : (i + 1) * band, :] = table(chunk)
        if side == 0:
            start_core(0)
    start_first(0)
    for turn in range(1, turns):
        start_core(turn)
        start_first(turn)
    for step, turn in (
        (start_gather, 0), (start_gather, 1), (start_share, 0), (start_gather, 2), (start_share, 1),
        (start_gather, 3), (start_out, 0), (start_share, 2), (start_out, 1), (start_share, 3),
        (start_hand, 0), (start_out, 2),
    ):
        step(turn)

    def factor(k, carry):
        def halfway():
            @pl.when(k == 0)
            def _():
                start_out(3)

            @pl.when(k + 1 < turns)
            def _():
                start_hand(k + 1)

        for copy in hand(k):
            copy().wait_recv()
        for place in range(turns):
            @pl.when(k == place)
            def _(place=place):
                gram_step(place)
        block[...] = pivot_rows(block[...], halfway)
        for place in range(turns):
            @pl.when(k == place)
            def _(place=place):
                row_step(place)
        return carry

    lax.fori_loop(0, turns, factor, 0)
    for copy in listed:
        copy().wait_send()

    def drain(t, carry):
        for copy in core(t) + first(t) + gathered(t) + shared(t) + out(t) + hand(t):
            copy().wait_send()
        return carry

    lax.fori_loop(0, turns, drain, 0)


def kernel_sketch(panel, signs, source_group, source_row, groups, devices):
    rows_here, columns = panel.shape
    per_owner = source_row.shape[2] // devices
    band = groups * devices * per_owner
    share = devices * per_owner
    turns = columns // BLOCK
    scale = 1.0 / math.sqrt(rows_here * devices * groups)
    vmem = pl.BlockSpec(memory_space=pltpu.VMEM)
    f32, bf16 = jnp.float32, jnp.bfloat16
    places = LISTS + SLOTS * turns
    return pl.pallas_call(
        functools.partial(sketch_kernel, groups, per_owner, scale, devices * band),
        out_shape=[
            jax.ShapeDtypeStruct((share, columns), f32),
            jax.ShapeDtypeStruct((columns, columns), bf16),
            jax.ShapeDtypeStruct((columns, columns), bf16),
        ],
        in_specs=[pl.BlockSpec(memory_space=pl.ANY)] + [vmem] * 3,
        out_specs=[vmem] * 3,
        scratch_shapes=[
            pltpu.VMEM((rows_here, columns), f32),
            pltpu.VMEM((2, devices, groups, share), jnp.int32),
            pltpu.VMEM((devices * groups, share), jnp.int32),
            pltpu.VMEM((turns, rows_here, 2 * BLOCK), bf16),
            pltpu.VMEM((devices * band, 1), jnp.int32),
            pltpu.VMEM((2, 4 * band, rows_here), bf16),
            pltpu.VMEM((turns, 4, band, BLOCK), f32),
            pltpu.VMEM((turns, 4, band, BLOCK), f32),
            pltpu.VMEM((turns, 4, band, BLOCK), f32),
            pltpu.VMEM((turns, 3, band, BLOCK), f32),
            pltpu.VMEM((turns, groups, share, BLOCK), f32),
            pltpu.VMEM((turns, devices, band, BLOCK), f32),
            pltpu.VMEM((devices * band, columns), bf16),
            pltpu.VMEM((devices * band, columns), bf16),
            pltpu.VMEM((BLOCK, BLOCK), f32),
            pltpu.VMEM((BLOCK, columns), f32),
            pltpu.SemaphoreType.DMA,
            pltpu.SemaphoreType.DMA((places,)),
            pltpu.SemaphoreType.DMA((places,)),
        ],
        compiler_params=pltpu.CompilerParams(collective_id=0, has_side_effects=True),
        name="sketch",
    )(
        panel,
        signs.reshape(rows_here // 128, 128),
        source_group.reshape(groups, share),
        source_row.reshape(groups, share),
    )


def apply_kernel(sketch_ref, high_ref, low_ref, panel_ref, own_ref, out_ref):
    @pl.when(pl.program_id(0) == 0)
    def _():
        own_ref[...] = sketch_ref[...]

    columns = panel_ref.shape[1]
    part = columns // 2
    panel = halves(panel_ref[...])
    for base in (0, part):
        deep = base + part
        factor = high_ref[base:deep, 0:deep], low_ref[base:deep, 0:deep]
        out_ref[:, base:deep] = split_matmul((panel[0][:, 0:deep], panel[1][:, 0:deep]), factor, ((1,), (1,)))


def apply_factor(sketch, high, low, panel):
    rows_here, columns = panel.shape
    part = 256
    fixed = lambda i: (0, 0)
    moving = pl.BlockSpec((part, columns), lambda i: (i, 0))
    once = pl.Buffered(1)
    return pl.pallas_call(
        apply_kernel,
        grid=(rows_here // part,),
        out_shape=[
            jax.ShapeDtypeStruct(sketch.shape, jnp.float32),
            jax.ShapeDtypeStruct(panel.shape, jnp.float32),
        ],
        in_specs=[
            pl.BlockSpec(sketch.shape, fixed, pipeline_mode=once),
            pl.BlockSpec(high.shape, fixed, pipeline_mode=once),
            pl.BlockSpec(low.shape, fixed, pipeline_mode=once),
            moving,
        ],
        out_specs=[pl.BlockSpec(sketch.shape, fixed), moving],
        name="apply",
    )(sketch, high, low, panel)


def bit_parity(value, bits):
    total = jnp.zeros_like(value)
    for bit_place in range(bits):
        total = total + (value >> bit_place & 1)
    return total & 1


def sylvester(order):
    index = jnp.arange(order, dtype=jnp.int32)
    parity = bit_parity(index[:, None] & index[None, :], order.bit_length())
    return (1 - 2 * parity).astype(jnp.float32)


def general_sketch(panel, signs, source_group, source_row):
    rows_here = panel.shape[0]
    columns = panel.shape[1]
    groups = lax.axis_size("grp")
    devices = lax.axis_size("dev")
    group_here = lax.axis_index("grp")
    highest = lax.Precision.HIGHEST
    flipped = panel * (1 - 2 * signs).astype(jnp.float32)[:, None]
    local = jnp.dot(
        sylvester(rows_here), flipped, precision=highest, preferred_element_type=jnp.float32
    )
    dev_table = sylvester(devices)
    mixed = jnp.einsum(
        "ed,dbc->ebc",
        dev_table,
        lax.all_to_all(
            local.reshape(devices, rows_here // devices, columns),
            "dev",
            split_axis=0,
            concat_axis=0,
            tiled=True,
        ),
        precision=highest,
    )
    inner = mixed
    inner = inner.reshape(rows_here, columns)
    chosen_group = source_group[:, 0, :, 0]
    chosen_row = source_row[:, 0, :]
    width = chosen_group.shape[1]
    per_owner = width // devices
    band_size = rows_here // devices
    dev_here = lax.axis_index("dev")
    stacked = jnp.stack([chosen_group, chosen_row]).reshape(2, groups, devices, per_owner)
    lists = lax.all_to_all(stacked, "dev", split_axis=2, concat_axis=2, tiled=True)
    band_group = lists[0].reshape(-1)
    band_row = lists[1].reshape(-1)
    flat_place = jnp.arange(groups * devices * per_owner, dtype=jnp.int32)
    source_dev = flat_place // per_owner % devices
    flat_index = source_dev * band_size + band_row - dev_here * band_size
    parity = bit_parity(band_group & group_here, groups.bit_length())
    factor = (1 - 2 * parity).astype(jnp.float32)
    gathered = lax.psum_scatter(
        inner[flat_index] * factor[:, None], "grp", scatter_dimension=0, tiled=True
    )
    panel_total = rows_here * devices * groups
    sketch = gathered * (1.0 / math.sqrt(panel_total))
    sketch_total = sketch.shape[0] * devices * groups
    partial_gram = jnp.dot(sketch.T, sketch, precision=highest, preferred_element_type=jnp.float32)
    return sketch, lax.psum(partial_gram, ("grp", "dev"))


def on_device(panel, signs, source_group, source_row):
    rows_here, columns = panel.shape
    groups = lax.axis_size("grp")
    devices = lax.axis_size("dev")
    width = source_row.shape[2]
    sketch_total = groups * devices * width
    fits = groups == 4 and devices == 8 and groups * width == BLOCK
    if fits and columns == 4 * BLOCK and rows_here % 256 == 0 and rows_here & (rows_here - 1) == 0:
        sketch, high, low = kernel_sketch(panel, signs, source_group, source_row, groups, devices)
        sketch, conditioned = apply_factor(sketch, high, low, panel)
        return (sketch, conditioned)
    sketch, gram = general_sketch(panel, signs, source_group, source_row)
    conditioned = pl.pallas_call(
        functools.partial(from_gram_kernel, sketch_total),
        out_shape=jax.ShapeDtypeStruct((rows_here, columns), jnp.float32),
        in_specs=[pl.BlockSpec(memory_space=pltpu.VMEM)] * 2,
        out_specs=pl.BlockSpec(memory_space=pltpu.VMEM),
        scratch_shapes=[pltpu.VMEM((columns, columns), jnp.float32)],
        name="factor",
    )(gram, panel)
    return (sketch, conditioned)


def solution(mesh):
    return jax.shard_map(
        on_device,
        mesh=mesh,
        in_specs=(
            P(("grp", "dev"), None),
            P(("grp", "dev")),
            P(None, "dev", None, None),
            P(None, "dev", None),
        ),
        out_specs=(P(("grp", "dev"), None), P(("grp", "dev"), None)),
        check_vma=False,
    )
```
